32 devices in a mesh: groups: 2 (over x), ffn: 16 (over z, y, core).
Axes of the slice: x: 2, y: 2, z: 4, core: 2. Of those that a mesh axis runs over, the one named last changes fastest.
Arguments:
- queries: bfloat16 [32, 2, 32, 1024], P(('groups', 'ffn')), parts along dimension 0, may hold values from -100 to 100
- block_kv: bfloat16 [32, 2, 32, 256], P(('groups', 'ffn')), parts along dimension 0, may hold values from -4 to 4
- cache_kv: bfloat16 [32, 2, 1536, 256], P(('groups', 'ffn')), parts along dimension 0, may hold values from -6 to 6
- prefix_len: int32 [8], P('groups'), parts along dimension 0, may hold values from 1 to 1536, as said below
- block_valid: int32 [8], P('groups'), parts along dimension 0, may hold values from 16 to 32, as said below
- resid: bfloat16 [32, 2, 32, 1024], P(('groups', 'ffn')), parts along dimension 0, may hold values from -6 to 6
- norm_gain: float32 [8192], replicated, may hold values from 0.25 to 1.75
- w_gate: bfloat16 [8192, 14336], P(None, 'ffn'), may hold values from -0.0625 to 0.0625
- w_up: bfloat16 [8192, 14336], P(None, 'ffn'), may hold values from -0.0625 to 0.0625
- w_down: bfloat16 [14336, 8192], P('ffn'), may hold values from -0.0625 to 0.0625
Outputs:
- layer_out: bfloat16 [32, 2, 32, 1024], P(('groups', 'ffn')), parts along dimension 0
The draws below stay inside these ranges and needn't reach their ends.
There are 2 independent parts, one for each index of `groups`. The reference program is written for one: setup_inputs(seed, part) draws one part's arguments, and reference() takes and returns one part's arrays. A program takes and returns all parts, laid end to end along the dimension named above; an argument that names none is the same for every part. Nothing has to cross between parts.
Inputs may be any that keep to these rules, and one draw needn't show every extreme that they name: `prefix_len`: some request has exactly 1536. `block_valid`: some request has exactly 32.
All inputs are finite; a program needn't handle non-finite values.
Results may differ from the reference program's by a relative error of at most 0.0061.
Values may be sent and summed in bfloat16 or wider, within the bound.
No kernel may reach another device: no remote copies, remote signals or barrier semaphores. Data moves between devices by JAX's collectives and lax.ppermute only.
A program may use at most 128 MiB of HBM per device.

```python
import jax
import jax.numpy as jnp
from jax import lax

KVH = 8
GQA = 8
HD = 128
FF = 14336
BLK = 32
LMAX = 1536
REQ_DEV = 2
D = 8192
SLOTS = 16
RGROUPS = 2
REQ = 4
TOKENS = 128


def joint_blocks(key):
    base_key = jax.random.fold_in(key, 11)
    query_key, block_key = jax.random.split(base_key)
    query_draw = jnp.clip(jax.random.normal(query_key, (SLOTS, REQ_DEV, BLK, GQA * HD), jnp.float32), -4.0, 4.0)
    block_draw = jnp.clip(jax.random.normal(block_key, (SLOTS, REQ_DEV, BLK, 2 * HD), jnp.float32), -4.0, 4.0)
    return (query_draw, block_draw)


def draw_queries(key, part):
    return joint_blocks(key)[0].astype(jnp.bfloat16)


def draw_block_kv(key, part):
    return joint_blocks(key)[1].astype(jnp.bfloat16)


def draw_prefix_len(key, part):
    first_key, second_key = jax.random.split(jax.random.fold_in(key, 23))
    lengths = jax.random.randint(first_key, (REQ,), 1, LMAX + 1).astype(jnp.int32)
    chosen = jax.random.randint(second_key, (), 0, REQ)
    return lengths.at[chosen].set(LMAX).astype(jnp.int32)


def draw_block_valid(key, part):
    first_key, second_key = jax.random.split(jax.random.fold_in(key, 37))
    counts = jax.random.randint(first_key, (REQ,), BLK // 2, BLK + 1).astype(jnp.int32)
    lower = jax.random.randint(second_key, (), BLK // 2, BLK).astype(jnp.int32)
    part_value = jnp.asarray(part, jnp.int32)
    full_index = jnp.asarray(part_value % REQ, jnp.int32)
    short_index = jnp.asarray((part_value + 1) % REQ, jnp.int32)
    counts = counts.at[short_index].set(lower)
    return counts.at[full_index].set(BLK).astype(jnp.int32)


def with_spikes(values, stream_key, source, target, shards_of, factor):
    def block_of(position):
        return (jnp.arange(values.shape[position]) // (values.shape[position] // shards_of)).reshape((-1,) + (1,) * (values.ndim - 1 - position))

    one_side = jax.random.permutation(stream_key, shards_of)[block_of(target)]
    second = (block_of(target) + shards_of // 2) % shards_of
    return jnp.where((block_of(source) == one_side) | (block_of(source) == second), factor * values, values)


def level_of(rng, extent, pieces, low, largest):
    loudness, own = 1.0, jax.random.fold_in(rng, 6)
    for axis_at, parts in pieces:
        heights = jnp.exp(jax.random.uniform(jax.random.fold_in(own, axis_at), (parts,), jnp.float32, low / len(pieces), largest / len(pieces)))
        loudness = loudness * jnp.repeat(heights, extent[axis_at] // parts).reshape([-1 if axis == axis_at else 1 for axis in range(len(extent))])
    return loudness


def scatter_about(rng, shape, scale, most, pieces=(), kind=jnp.bfloat16):
    result = scale * jax.random.normal(rng, shape, jnp.float32)
    if pieces:
        result = result * level_of(rng, shape, pieces, -0.22, 0.18)
    return jnp.clip(result, -most, most).astype(kind)


def bell_draw_with(key, extent, scale, reach, cuts, heavy, kind=jnp.bfloat16):
    drawn = scale * jax.random.normal(key, extent, jnp.float32)
    if cuts:
        drawn = drawn * level_of(key, extent, cuts, -0.22, 0.18)
    return jnp.clip(with_spikes(drawn, jax.random.fold_in(key, 3), *heavy), -reach, reach).astype(kind)


def setup_inputs(seed: int = 0, part: int = 0) -> dict:
    key_of = jax.random.split(jax.random.key(seed), 11)
    part_splits = jax.random.split(jax.random.fold_in(key_of[10], part), 11)
    queries = draw_queries(jax.random.fold_in(jax.random.fold_in(key_of[10], part), 71), part)
    block_kv = draw_block_kv(jax.random.fold_in(jax.random.fold_in(key_of[10], part), 71), part)
    cache_kv = scatter_about(part_splits[2], (SLOTS, REQ_DEV, LMAX, 2 * HD), 1.0, 6.0, ((0, 16),))
    prefix_len = draw_prefix_len(jax.random.fold_in(jax.random.fold_in(key_of[10], part), 71), part)
    block_valid = draw_block_valid(jax.random.fold_in(jax.random.fold_in(key_of[10], part), 71), part)
    resid = scatter_about(part_splits[5], (SLOTS, REQ_DEV, BLK, GQA * HD), 1.0, 6.0, ((0, 16),))
    norm_gain = jnp.clip(1.0 + 0.15 * jax.random.normal(key_of[6], (D,), jnp.float32), 0.25, 1.75)
    w_gate = scatter_about(key_of[7], (D, FF), D ** -0.5, 0.0625, ((1, 16),))
    w_up = scatter_about(key_of[8], (D, FF), D ** -0.5, 0.0625, ((1, 16),))
    w_down = bell_draw_with(key_of[9], (FF, D), FF ** -0.5, 0.0625, ((0, 16),), (0, 1, 16, 2.0))
    return dict(queries=queries, block_kv=block_kv, cache_kv=cache_kv, prefix_len=prefix_len, block_valid=block_valid, resid=resid, norm_gain=norm_gain, w_gate=w_gate, w_up=w_up, w_down=w_down)


def attend_all(queries, block_kv, cache_kv, prefix_here, valid_here):
    slot_count = queries.shape[0]
    keys_all = jnp.concatenate([cache_kv[..., :HD], block_kv[..., :HD]], axis=2).astype(jnp.float32)
    values_all = jnp.concatenate([cache_kv[..., HD:], block_kv[..., HD:]], axis=2).astype(jnp.float32)
    positions = jnp.arange(LMAX + BLK)
    visible = jnp.where(positions[None, None, :] < LMAX, positions[None, None, :] < prefix_here[:, :, None], positions[None, None, :] - LMAX < valid_here[:, :, None])
    query_heads = queries.astype(jnp.float32).reshape(slot_count, REQ_DEV, BLK, GQA, HD)
    scores = jnp.einsum('srbgd,srkd->srgbk', query_heads, keys_all) * (1.0 / jnp.sqrt(jnp.float32(HD)))
    masked = jnp.where(visible[:, :, None, None, :], scores, jnp.float32(-1e+30))
    peak = lax.optimization_barrier(jnp.max(masked, axis=-1, keepdims=True))
    exps = jnp.exp(masked - peak)
    totals = lax.optimization_barrier(jnp.sum(exps, axis=-1, keepdims=True))
    probability = (exps / totals).astype(jnp.bfloat16)
    mixed = jnp.einsum('srgbk,srkd->srbgd', probability.astype(jnp.float32), values_all)
    return mixed.reshape(slot_count, REQ_DEV, BLK, GQA * HD)

def reference(queries, block_kv, cache_kv, prefix_len, block_valid, resid, norm_gain, w_gate, w_up, w_down):
    width = GQA * HD
    slot_request = ((jnp.arange(SLOTS) // KVH)[:, None] * REQ_DEV + jnp.arange(REQ_DEV)[None, :]).astype(jnp.int32)
    prefix_here = prefix_len[slot_request]
    valid_here = block_valid[slot_request]
    attended = attend_all(queries, block_kv, cache_kv, prefix_here, valid_here)
    mid_state = (resid.astype(jnp.float32) + attended).astype(jnp.bfloat16)
    mid_split = mid_state.astype(jnp.float32).reshape(RGROUPS, KVH, REQ_DEV, BLK, width)
    mean_square = lax.optimization_barrier(jnp.sum(mid_split * mid_split, axis=(1, 4))) / D
    inv_root = lax.rsqrt(mean_square + 1e-05)
    gain_split = norm_gain.reshape(KVH, width)[None, :, None, None, :]
    normed = (mid_split * inv_root[:, None, :, :, None] * gain_split).astype(jnp.bfloat16)
    token_rows = jnp.transpose(normed, (0, 2, 3, 1, 4)).reshape(TOKENS, D)
    gate_proj = jnp.dot(token_rows, w_gate, preferred_element_type=jnp.float32)
    up_proj = jnp.dot(token_rows, w_up, preferred_element_type=jnp.float32)
    hidden = (jax.nn.silu(gate_proj) * up_proj).astype(jnp.bfloat16)
    ffn_sum = jnp.dot(hidden, w_down, preferred_element_type=jnp.float32)
    ffn_split = jnp.transpose(ffn_sum.reshape(RGROUPS, REQ_DEV, BLK, KVH, width), (0, 3, 1, 2, 4))
    ffn_split = ffn_split.reshape(SLOTS, REQ_DEV, BLK, width)
    return (mid_state.astype(jnp.float32) + ffn_split).astype(jnp.bfloat16)
```

```python
import jax
import jax.numpy as jnp
from jax import lax
from jax.sharding import PartitionSpec as P

KVH = 8
epsilon = 1e-05


def attend_local(queries, block_kv, cache_kv, prefix_here, valid_here):
    slot_count = queries.shape[0]
    request_count = queries.shape[1]
    block_len = queries.shape[2]
    cache_len = cache_kv.shape[2]
    head_size = block_kv.shape[3] // 2
    query_count = queries.shape[3] // head_size
    keys_all = jnp.concatenate([cache_kv[..., :head_size], block_kv[..., :head_size]], axis=2)
    values_all = jnp.concatenate([cache_kv[..., head_size:], block_kv[..., head_size:]], axis=2)
    positions = jnp.arange(cache_len + block_len)
    visible = jnp.where(
        positions[None, None, :] < cache_len,
        positions[None, None, :] < prefix_here[:, :, None],
        positions[None, None, :] - cache_len < valid_here[:, :, None],
    )
    query_heads = queries.reshape(slot_count, request_count, block_len, query_count, head_size)
    scores = jnp.einsum(
        "srbgd,srkd->srgbk", query_heads, keys_all, preferred_element_type=jnp.float32
    )
    scores = scores * (1.0 / jnp.sqrt(jnp.float32(head_size)))
    masked = jnp.where(visible[:, :, None, None, :], scores, jnp.float32(-1e30))
    peak = jnp.max(masked, axis=-1, keepdims=True)
    exps = jnp.exp(masked - peak)
    totals = jnp.sum(exps, axis=-1, keepdims=True)
    probability = (exps / totals).astype(jnp.bfloat16)
    mixed = jnp.einsum(
        "srgbk,srkd->srbgd", probability, values_all, preferred_element_type=jnp.float32
    )
    return mixed.reshape(slot_count, request_count, block_len, query_count * head_size)


def exchange(value, bit, count):
    return lax.ppermute(value, "ffn", [(i, i ^ bit) for i in range(count)])


def joined(mine, theirs, high, axis):
    first = jnp.where(high, theirs, mine)
    second = jnp.where(high, mine, theirs)
    return jnp.stack([first, second], axis=axis)


def gather_rows(mid, me, count):
    rows, width = mid.shape
    value = mid
    bit = KVH
    while bit < count:
        other = exchange(value, bit, count)
        value = joined(value, other, (me & bit) != 0, 0).reshape(-1, width)
        bit *= 2
    total = value.shape[0]
    half = width // 2
    left, right = value[:, :half], value[:, half:]
    left1 = joined(left, exchange(left, 4, count), (me & 4) != 0, 0)
    right1 = joined(right, exchange(right, 2, count), (me & 2) != 0, 0)
    left2 = joined(left1, exchange(left1, 2, count), (me & 2) != 0, 1)
    right2 = joined(right1, exchange(right1, 4, count), (me & 4) != 0, 0)
    both = jnp.stack([left2, right2], axis=2)
    whole = joined(both, exchange(both, 1, count), (me & 1) != 0, 2)
    return jnp.transpose(whole, (4, 0, 1, 2, 3, 5)).reshape(total, KVH * width)


def halves(value, high, axis):
    first = lax.index_in_dim(value, 0, axis, keepdims=False)
    second = lax.index_in_dim(value, 1, axis, keepdims=False)
    return jnp.where(high, second, first), jnp.where(high, first, second)


def reduce_step(value, bit, axis, me, count):
    keep, send = halves(value, (me & bit) != 0, axis)
    return keep + exchange(send.astype(jnp.bfloat16), bit, count).astype(jnp.float32)


def scatter_sum(partial, me, count):
    total = partial.shape[0]
    width = partial.shape[1] // KVH
    half = width // 2
    value = partial.reshape(total, 2, 2, 2, width)
    value = reduce_step(value, 1, 3, me, count)
    left, right = value[..., :half], value[..., half:]
    left = reduce_step(left, 2, 2, me, count)
    right = reduce_step(right, 4, 1, me, count)
    left = reduce_step(left, 4, 1, me, count)
    right = reduce_step(right, 2, 1, me, count)
    value = jnp.concatenate([left, right], axis=1)
    bit = count // 2
    while bit >= KVH:
        value = reduce_step(value.reshape(2, -1, width), bit, 0, me, count)
        bit //= 2
    return value


def body(
    queries, block_kv, cache_kv, prefix_len, block_valid, resid, norm_gain, w_gate, w_up, w_down
):
    axis_count = lax.axis_size("ffn")
    device_index = lax.axis_index("ffn")
    group_index = device_index // KVH
    request_count = queries.shape[1]
    width = queries.shape[3]
    model_width = KVH * width
    prefix_here = lax.dynamic_slice_in_dim(prefix_len, group_index * request_count, request_count)[
        None, :
    ]
    valid_here = lax.dynamic_slice_in_dim(block_valid, group_index * request_count, request_count)[
        None, :
    ]
    attended = attend_local(queries, block_kv, cache_kv, prefix_here, valid_here)
    mid_state = (resid.astype(jnp.float32) + attended).astype(jnp.bfloat16)
    tokens = gather_rows(mid_state.reshape(-1, width), device_index, axis_count)
    tokens = tokens.astype(jnp.float32)
    mean_square = jnp.sum(tokens * tokens, axis=1, keepdims=True) / model_width
    normed = (tokens * lax.rsqrt(mean_square + epsilon) * norm_gain[None, :]).astype(jnp.bfloat16)
    gate_proj = jnp.dot(normed, w_gate, preferred_element_type=jnp.float32)
    up_proj = jnp.dot(normed, w_up, preferred_element_type=jnp.float32)
    hidden = (jax.nn.silu(gate_proj) * up_proj).astype(jnp.bfloat16)
    partial = jnp.dot(hidden, w_down, preferred_element_type=jnp.float32)
    ffn_sum = scatter_sum(partial, device_index, axis_count)
    return (mid_state.astype(jnp.float32) + ffn_sum.reshape(resid.shape)).astype(jnp.bfloat16)


def solution(mesh):
    in_specs = (
        P(("groups", "ffn"), None, None, None),
        P(("groups", "ffn"), None, None, None),
        P(("groups", "ffn"), None, None, None),
        P("groups"),
        P("groups"),
        P(("groups", "ffn"), None, None, None),
        P(),
        P(None, "ffn"),
        P(None, "ffn"),
        P("ffn", None),
    )
    out_specs = P(("groups", "ffn"), None, None, None)
    return jax.shard_map(body, mesh=mesh, in_specs=in_specs, out_specs=out_specs, check_vma=False)
```
